256 devices in a mesh: expert: 64 (over x, z, y_lo), dp: 4 (over y_hi, core).
Axes of the slice: x: 4, y: 4 (y_hi: 2, y_lo: 2; y = y_hi * 2 + y_lo), z: 8, core: 2. Of those that a mesh axis runs over, the one named last changes fastest.
Arguments:
- tokens: bfloat16 [32768, 2048], P(('expert', 'dp')), may hold values from -6 to 6
- cotangent: bfloat16 [32768, 2048], P(('expert', 'dp')), may hold values from -6 to 6
- expert_ids: int32 [32768, 2], P(('expert', 'dp')), may hold values from 0 to 63, all different within a row; in each aligned block of 128 rows (0 to 127, 128 to 255, ...) at most 6 rows name the same one
- gate_probs: bfloat16 [32768, 2], P(('expert', 'dp')), may hold values from 0.019897461 to 0.29882812
- weights: bfloat16 [64, 2048, 1152], P('expert', 'dp'), may hold values from -6 to 6
- first_moment: float32 [64, 2048, 1152], P('expert', 'dp'), may hold values from -4 to 4
- second_moment: float32 [64, 2048, 1152], P('expert', 'dp'), may hold values from 0.01 to 1
- swap_flags: int32 [64], P('expert'), may hold values from 0 to 1, as said below
Outputs:
- token_grads: bfloat16 [32768, 2048], P(('expert', 'dp'))
- gate_grads: bfloat16 [32768, 2], P(('expert', 'dp'))
- new_weights: bfloat16 [64, 2048, 1152], P('expert', 'dp')
- new_first: float32 [64, 2048, 1152], P('expert', 'dp')
- new_second: float32 [64, 2048, 1152], P('expert', 'dp')
The draws below stay inside these ranges and needn't reach their ends.
Inputs may be any that keep to these rules, and one draw needn't show every extreme that they name: `expert_ids`: among the 256 choices of one device's tokens at most 6 name one expert, and in every draw some device sends exactly 6 to some expert; a token's 2 experts differ. swap_flags[i] equals swap_flags[i XOR 64/2].
All inputs are finite; a program needn't handle non-finite values.
Results may differ from the reference program's by a relative error of at most 0.0072.
Values may be sent and summed in bfloat16 or wider, within the bound.
A program may use at most 128 MiB of HBM per device.

```python
import math
import jax
import jax.numpy as jnp
import numpy as np
from jax import lax

D = 2048
HID = 384
TOPK = 2
TOK_DEV = 128
EXPERTS = 64
CAP = 6
TOKENS = 32768
N_EXPERT = 64
N_DP = 4


def draw_swap_flags(key, part):
    half_flags = jax.random.randint(jax.random.fold_in(key, 17), (EXPERTS // 2,), 0, 2).astype(jnp.int32)
    return jnp.concatenate([half_flags, half_flags])


def shard_levels(own_key, extent, shards, smallest, high):
    factor_of, own = 1.0, jax.random.fold_in(own_key, 6)
    for dim, parts in shards:
        steps = jnp.exp(jax.random.uniform(jax.random.fold_in(own, dim), (parts,), jnp.float32, smallest / len(shards), high / len(shards)))
        factor_of = factor_of * jnp.repeat(steps, extent[dim] // parts).reshape([-1 if axis == dim else 1 for axis in range(len(extent))])
    return factor_of


def routed_block(own_key, own, number, rows, number_of, top, reach, skew):
    ranking = jax.random.permutation(own_key, number_of)
    crowded, common = portions_of(number_of, rows * top, reach, skew, True), portions_of(number_of, rows * top, reach, skew, False)
    places = jnp.arange(number_of)

    def named(tallies, rotation):
        used = int((tallies > 0).sum())
        fixed = max(1, used // 4)
        shifted = fixed + (places - fixed + rotation * (used - fixed)) % max(1, number_of - fixed)
        return jnp.zeros((number_of,), jnp.int32).at[ranking[jnp.where(places < fixed, places, shifted)]].set(jnp.asarray(tallies, jnp.int32))

    tallies = jnp.where(number % 4 == 0, named(crowded, number // 4), named(common, number - number // 4 - 1))
    mixed = jax.random.permutation(jax.random.fold_in(own, 3), number_of)
    giver, taker = mixed[0:number_of // 2 * 2:2], mixed[1:number_of // 2 * 2:2]
    slack = jnp.minimum(tallies[giver] - 1, reach - tallies[taker]) // 2
    slack = jnp.where((giver == ranking[0]) | (taker == ranking[0]) | (tallies[taker] == 0), 0, jnp.maximum(slack, 0))
    shifted = jax.random.randint(jax.random.fold_in(own, 4), (number_of // 2,), 0, 1 << 20) % (slack + 1)
    tallies = tallies.at[giver].add(-shifted).at[taker].add(shifted)
    items = jnp.searchsorted(jnp.cumsum(tallies), jnp.arange(rows * top), side="right").astype(jnp.int32)
    grid = items.reshape(top, rows).T
    grid = grid[jax.random.permutation(jax.random.fold_in(own, 1), rows)]
    rotation = jax.random.randint(jax.random.fold_in(own, 2), (rows, 1), 0, top)
    return jnp.take_along_axis(grid, (jnp.arange(top)[None, :] + rotation) % top, axis=1)


def portions_of(count, total, bound, lean, full):
    loads = [(1 << 20) // math.isqrt(standing ** lean) + 1 for standing in range(1, count + 1)]
    largest = bound if full else min(bound, max(-(-total // count), total * loads[0] // sum(loads)))
    least = 1 if total - largest >= count - 1 else 0
    given, surplus = [largest] + [least] * (count - 1), total - largest - least * (count - 1)
    while surplus > 0:
        free = [i for i in range(1, count) if given[i] < largest] or [i for i in range(1, count) if given[i] < bound]
        mass, left = sum([loads[i] for i in free]), surplus
        for i in free:
            addition = min(bound - given[i], max(1, left * loads[i] // mass), surplus)
            given[i] = given[i] + addition
            surplus = surplus - addition
    return np.array(given)


def normal_values(rng, shape, spread, reach, shards=(), held_as=jnp.bfloat16):
    entries = spread * jax.random.normal(rng, shape, jnp.float32)
    if shards:
        entries = entries * shard_levels(rng, shape, shards, -0.22, 0.18)
    return jnp.clip(entries, -reach, reach).astype(held_as)


def setup_inputs(seed: int = 0) -> dict:
    seeds = jax.random.split(jax.random.key(seed), 9)
    tokens = normal_values(seeds[0], (TOKENS, D), 1.0, 6.0, ((0, 256),))
    cotangent = normal_values(seeds[1], (TOKENS, D), 1.0, 6.0, ((0, 256),))
    expert_ids_keys = jax.random.split(jax.random.fold_in(seeds[2], 1), TOKENS // TOK_DEV)
    expert_ids_turns = jax.random.permutation(jax.random.fold_in(seeds[2], 3), TOKENS // TOK_DEV)
    expert_ids = jax.vmap(lambda own, number: routed_block(jax.random.fold_in(seeds[2], 2), own, number, TOK_DEV, EXPERTS, TOPK, CAP, 2))(expert_ids_keys, expert_ids_turns).reshape((TOKENS, TOPK))
    gate_probs = jnp.clip(0.019897461 + 0.27893066 * jax.random.uniform(seeds[3], (TOKENS, TOPK), jnp.float32) ** shard_levels(seeds[3], (TOKENS, TOPK), ((0, 256),), -0.2, 0.2), 0.019897461, 0.29882812).astype(jnp.bfloat16)
    weights = normal_values(seeds[4], (EXPERTS, D, 3 * HID), 1.0, 6.0, ((0, 64), (1, 4)))
    first_moment = normal_values(seeds[5], (EXPERTS, D, 3 * HID), 0.3, 4.0, ((0, 64), (1, 4)), jnp.float32)
    second_moment = jnp.clip(jnp.exp(math.log(1.0) - 4.6051702 * jax.random.uniform(seeds[6], (EXPERTS, D, 3 * HID), jnp.float32) ** shard_levels(seeds[6], (EXPERTS, D, 3 * HID), ((0, 64), (1, 4)), -0.2, 0.2)), 0.01, 1.0)
    swap_flags = draw_swap_flags(jax.random.fold_in(seeds[8], 71), 0)
    return {"tokens": tokens, "cotangent": cotangent, "expert_ids": expert_ids, "gate_probs": gate_probs, "weights": weights, "first_moment": first_moment, "second_moment": second_moment, "swap_flags": swap_flags}


bias_first = 1.0 - 0.9 ** 20
bias_second = 1.0 - 0.95 ** 20

def reference(tokens, cotangent, expert_ids, gate_probs, weights, first_moment, second_moment, swap_flags):
    scale_in = 1.0 / math.sqrt(D)
    scale_out = 1.0 / math.sqrt(HID)
    slot_total = TOKENS * TOPK
    flat_ids = expert_ids.reshape(-1)
    owner = jnp.arange(slot_total, dtype=jnp.int32) // TOPK
    replica = owner // TOK_DEV % N_DP
    flat_probs = gate_probs.reshape(-1)
    rows_most = N_EXPERT * CAP
    positions = jnp.arange(rows_most, dtype=jnp.int32)

    def per_expert(carry, expert):
        grad_acc, score_acc = carry
        full = weights[expert]
        w_in = full[:, :2 * HID]
        w_down = full[:, 2 * HID:]
        total = jnp.zeros((D, 3 * HID), jnp.float32)
        for rep in range(N_DP):
            chosen = (flat_ids == expert) & (replica == rep)
            found = jnp.sum(chosen.astype(jnp.int32))
            index, = jnp.nonzero(chosen, size=rows_most, fill_value=0)
            index = index.astype(jnp.int32)
            valid = positions < found
            tok = owner[index]
            rows = jnp.where(valid[:, None], tokens[tok], jnp.zeros((), jnp.bfloat16))
            cots = jnp.where(valid[:, None], cotangent[tok], jnp.zeros((), jnp.bfloat16))
            probs = jnp.where(valid, flat_probs[index], jnp.zeros((), jnp.bfloat16))
            pre = (jnp.dot(rows, w_in, preferred_element_type=jnp.float32) * scale_in).astype(jnp.bfloat16)
            pre = lax.optimization_barrier(pre).astype(jnp.float32)
            gate = pre[:, :HID]
            upper = pre[:, HID:]
            sig = jax.nn.sigmoid(gate)
            active = (gate * sig * upper).astype(jnp.bfloat16)
            result = lax.dot_general(active, w_down, (((1,), (1,)), ((), ())), preferred_element_type=jnp.float32) * scale_out
            score = lax.optimization_barrier(jnp.sum(cots.astype(jnp.float32) * result, axis=1)).astype(jnp.bfloat16)
            d_out = (probs[:, None].astype(jnp.float32) * cots.astype(jnp.float32)).astype(jnp.bfloat16)
            d_active = jnp.dot(d_out, w_down, preferred_element_type=jnp.float32) * scale_out
            d_gate = d_active * upper * sig * (1.0 + gate * (1.0 - sig))
            d_upper = d_active * gate * sig
            d_pre = jnp.concatenate([d_gate, d_upper], axis=1).astype(jnp.bfloat16)
            d_row = (lax.dot_general(d_pre, w_in, (((1,), (1,)), ((), ())), preferred_element_type=jnp.float32) * scale_in).astype(jnp.bfloat16)
            d_row = lax.optimization_barrier(d_row).astype(jnp.float32)
            g_in = lax.dot_general(rows, d_pre, (((0,), (0,)), ((), ())), preferred_element_type=jnp.float32) * scale_in
            g_down = lax.dot_general(d_out, active, (((0,), (0,)), ((), ())), preferred_element_type=jnp.float32) * scale_out
            partial_grad = jnp.concatenate([g_in, g_down], axis=1).astype(jnp.bfloat16)
            total = total + lax.optimization_barrier(partial_grad).astype(jnp.float32)
            grad_acc = grad_acc.at[tok].add(jnp.where(valid[:, None], d_row, jnp.float32(0.0)))
            score_acc = score_acc.at[index].add(jnp.where(valid, score.astype(jnp.float32), jnp.float32(0.0)))
        return ((grad_acc, score_acc), total)
    start = (jnp.zeros((TOKENS, D), jnp.float32), jnp.zeros((slot_total,), jnp.float32))
    (grad_acc, score_acc), grads = lax.scan(per_expert, start, jnp.arange(EXPERTS, dtype=jnp.int32))
    token_grads = grad_acc.astype(jnp.bfloat16)
    gate_grads = score_acc.reshape(TOKENS, TOPK).astype(jnp.bfloat16)
    moment = 0.9 * first_moment + 0.1 * grads
    square = 0.95 * second_moment + 0.05 * grads * grads
    update = moment / bias_first / (jnp.sqrt(square / bias_second) + 1e-08)
    old = weights.astype(jnp.float32)
    fresh = (old - 0.02 * (update + 0.1 * old)).astype(jnp.bfloat16)
    partner = jnp.bitwise_xor(jnp.arange(EXPERTS, dtype=jnp.int32), EXPERTS // 2)
    flag = (swap_flags != 0)[:, None, None]
    new_weights = jnp.where(flag, fresh[partner], fresh)
    new_first = jnp.where(flag, moment[partner], moment)
    new_second = jnp.where(flag, square[partner], square)
    return (token_grads, gate_grads, new_weights, new_first, new_second)
```

```python
import math

import jax
import jax.numpy as jnp
from jax import lax
from jax.experimental import pallas as pl
from jax.experimental.pallas import tpu as pltpu
from jax.sharding import PartitionSpec as P

bias_first = 1.0 - 0.9**20
bias_second = 1.0 - 0.95**20
MESH = pl.DeviceIdType.MESH
f32 = jnp.float32
bf16 = jnp.bfloat16

NX, NZ, NY = 4, 8, 2
CAP = 6
GROUP = 8
BLK = GROUP * CAP
ROWS = GROUP * BLK
D = 2048
HID = 384
TOK = 128
HALF = 1024
OWN = 512
SCALE_IN = 1.0 / math.sqrt(D)
SCALE_OUT = 1.0 / math.sqrt(HID)
Z_ORDER = (4, 3, 5, 2, 6, 1, 7)
XY_ORDER = ((2, 1), (2, 0), (1, 1), (3, 1), (1, 0), (3, 0), (0, 1))


def step_kernel(
    pick, pick_prob, tok, cot, w_own, flag, plain, trade, m_hbm, v_hbm,
    tg, score_out, g_sum, g_recv, w_recv, m_recv, v_recv,
    z_send, z_recv, xy_send, xy_recv, w_full, flags, perm,
    pre, d_act, active, d_pre,
    ret_a, ret_b, rxy_a, rxy_b, rz_a, rz_b, back_a, back_b,
    g_part, c_recv, g_send, stage, m_bf, v_bf,
    zs, zr, xs, xr, fs, fr, rxs, rxr, rzs, rzr, ws, wr, ms, mr, gs, gr, ls,
):
    e = lax.axis_index("expert")
    dp = lax.axis_index("dp")
    x = e // (NZ * NY)
    z = (e // NY) % NZ
    y = e % NY
    p = x * NY + y
    core_mate = dp + 1 - 2 * (dp % 2)
    y_mate = (dp + 2) % 4
    diag_mate = (core_mate + 2) % 4

    def at(nx, nz, ny, nd):
        return (nx * (NZ * NY) + nz * NY + ny, nd)

    def z_dev(k):
        return at(x, (z + k) % NZ, y, dp)

    def xy_pos(k, ky):
        return (x + k) % NX, (y + ky) % NY

    def xy_dev(k, ky):
        nx, ny = xy_pos(k, ky)
        return at(nx, z, ny, dp)

    partner = at((x + 2) % NX, z, y, dp)

    def remote(src, dst, ssem, rsem, device):
        return pltpu.make_async_remote_copy(
            src_ref=src, dst_ref=dst, send_sem=ssem, recv_sem=rsem,
            device_id=device, device_id_type=MESH,
        )

    m_in = pltpu.make_async_copy(m_hbm, stage.at[0], ls.at[0])
    v_in = pltpu.make_async_copy(v_hbm, stage.at[1], ls.at[1])
    m_in.start()
    v_in.start()

    barrier = pltpu.get_barrier_semaphore()
    targets = [z_dev(k) for k in Z_ORDER]
    targets += [xy_dev(*k) for k in XY_ORDER]
    targets += [(e, core_mate), (e, y_mate)]
    for device in targets:
        pl.semaphore_signal(barrier, inc=1, device_id=device, device_id_type=MESH)

    def fill(c):
        sel = pick if c < 2 else pick_prob
        src = tok if c < 2 else cot

        @pl.loop(0, HALF // 256)
        def _(i):
            cols = pl.ds(pl.multiple_of(i * 256, 256), 256)
            scols = pl.ds(pl.multiple_of((c % 2) * HALF + i * 256, 256), 256)
            out = jnp.dot(sel[...], src[:, scols], preferred_element_type=f32)
            z_send[c, :, :, cols] = out.astype(bf16).reshape(GROUP, BLK, 256)

    fill(0)
    pl.semaphore_wait(barrier, len(targets))

    copies = []

    def start(c):
        c.start()
        copies.append(c)
        return c

    def z_stage(src, dst, ssem, rsem):
        out = []
        for i, k in enumerate(Z_ORDER):
            out.append(start(remote(
                src.at[(z + k) % NZ], dst.at[z], ssem.at[i], rsem.at[i], z_dev(k))))
        return out

    def xy_stage(src, dst, ssem, rsem):
        out = []
        for i, k in enumerate(XY_ORDER):
            nx, ny = xy_pos(*k)
            out.append(start(remote(
                src.at[nx * NY + ny], dst.at[p], ssem.at[i], rsem.at[i], xy_dev(*k))))
        return out

    z_copies = [z_stage(z_send.at[0], z_recv.at[0], zs.at[0], zr.at[0])]
    w_x = start(remote(w_own, w_recv, ws.at[0], wr.at[0], partner))
    flag_copies = []
    for i, k in enumerate(XY_ORDER):
        flag_copies.append(start(remote(
            flag.at[:, pl.ds(0, ROWS)], flags.at[p], fs.at[i], fr.at[i], xy_dev(*k))))
    for c in range(1, 4):
        fill(c)
        z_copies.append(z_stage(z_send.at[c], z_recv.at[c], zs.at[c], zr.at[c]))

    flags[p] = flag[:, pl.ds(0, ROWS)]
    for c in range(4):
        z_recv[c, z] = z_send[c, z]
    for c in flag_copies:
        c.wait_recv()
    for q in range(GROUP):
        rows = pl.ds(q * BLK, BLK)
        f = flags[q, 0:1, :]
        a = plain[rows, :].astype(f32)
        b = trade[rows, :].astype(f32)
        perm[rows, :] = (a + (b - a) * f).astype(bf16)

    def permute(src, dst, width, forward):
        dims = ((1,), (0,)) if forward else ((0,), (0,))

        def tile(start_col, n):
            cols = pl.ds(start_col, n)
            block = src[:, :, cols].reshape(ROWS, n)
            out = lax.dot_general(perm[...], block, (dims, ((), ())), preferred_element_type=f32)
            dst[:, :, cols] = out.astype(bf16).reshape(GROUP, BLK, n)

        @pl.loop(0, width // 256)
        def _(i):
            tile(pl.multiple_of(i * 256, 256), 256)

        if width % 256:
            tile(width - width % 256, width % 256)

    xy_copies = [None] * 4

    def dispatch(c):
        for cp in z_copies[c]:
            cp.wait_recv()
        permute(z_recv.at[c], xy_send.at[c], HALF, True)
        xy_copies[c] = xy_stage(xy_send.at[c], xy_recv.at[c], xs.at[c], xr.at[c])
        xy_recv[c, p] = xy_send[c, p]

    dispatch(0)

    w_x.wait_recv()

    @pl.loop(0, OWN // 32)
    def _(i):
        rows = pl.ds(pl.multiple_of(i * 32, 32), 32)
        f = flag[0:1, :]
        mine = w_own[rows, :].astype(f32)
        other = w_recv[rows, :].astype(f32)
        w_full[dp, rows, :] = jnp.where(f != 0.0, other, mine).astype(bf16)

    w_y = start(remote(w_full.at[dp], w_full.at[dp], ws.at[1], wr.at[1], (e, y_mate)))
    w_c = start(remote(w_full.at[dp], w_full.at[dp], ws.at[2], wr.at[2], (e, core_mate)))

    def send_moment(slot, local, buf, dst):
        local.wait()

        @pl.loop(0, OWN // 32)
        def _(i):
            rows = pl.ds(pl.multiple_of(i * 32, 32), 32)
            buf[rows, :] = stage[slot, rows, :].astype(bf16)

        return start(remote(buf, dst, ms.at[slot], mr.at[slot], partner))

    dispatch(1)
    m_x = send_moment(0, m_in, m_bf, m_recv)
    dispatch(2)
    w_y.wait_recv()
    w_f = start(remote(w_full.at[y_mate], w_full.at[y_mate], ws.at[3], wr.at[3], (e, core_mate)))
    w_c.wait_recv()
    w_f.wait_recv()
    for c in (0, 1):
        for cp in xy_copies[c]:
            cp.wait_recv()

    def x_block(c, cols):
        return xy_recv[c, :, :, cols].reshape(ROWS, cols.size)

    @pl.loop(0, 3)
    def _(i):
        cols = pl.ds(pl.multiple_of(i * 256, 256), 256)
        acc = jnp.zeros((ROWS, 256), f32)
        for b in range(4):
            acc += jnp.dot(
                x_block(b // 2, pl.ds((b % 2) * OWN, OWN)), w_full[b, :, cols],
                preferred_element_type=f32)
        pre[:, cols] = (acc * SCALE_IN).astype(bf16)

    @pl.loop(0, GROUP)
    def _(i):
        rows = pl.ds(pl.multiple_of(i * BLK, BLK), BLK)
        g = pre[rows, 0:HID].astype(f32)
        u = pre[rows, HID : 2 * HID].astype(f32)
        s = 1.0 / (1.0 + jnp.exp(-g))
        active[rows, :] = (g * s * u).astype(bf16)

    dispatch(3)

    def act_part(c):
        for cp in xy_copies[c]:
            cp.wait_recv()

        @pl.loop(0, 2)
        def _(r):
            rows = pl.ds(pl.multiple_of(r * (ROWS // 2), ROWS // 2), ROWS // 2)
            acc = jnp.zeros((ROWS // 2, HID), f32)
            for b in (2 * (c % 2), 2 * (c % 2) + 1):
                block = xy_recv[c, pl.ds(r * 4, 4), :, pl.ds((b % 2) * OWN, OWN)]
                acc += jnp.dot(
                    block.reshape(ROWS // 2, OWN), w_full[b, :, 2 * HID : 3 * HID],
                    preferred_element_type=f32)
            if c == 2:
                d_act[rows, :] = acc
            else:
                d_act[rows, :] += acc

    act_part(2)
    act_part(3)

    lane = lax.broadcasted_iota(jnp.int32, (BLK, 128), 1)

    @pl.loop(0, GROUP)
    def _(i):
        rows = pl.ds(pl.multiple_of(i * BLK, BLK), BLK)
        g = pre[rows, 0:HID].astype(f32)
        u = pre[rows, HID : 2 * HID].astype(f32)
        s = 1.0 / (1.0 + jnp.exp(-g))
        da = d_act[rows, :] * SCALE_OUT
        sc = jnp.sum(active[rows, :].astype(f32) * da, axis=1, keepdims=True)
        d_pre[rows, 0:HID] = (da * u * s * (1.0 + g * (1.0 - s))).astype(bf16)
        d_pre[rows, HID : 2 * HID] = (da * g * s).astype(bf16)
        high = jnp.broadcast_to(sc, (BLK, 128)).astype(bf16)
        low = (jnp.broadcast_to(sc, (BLK, 128)) - high.astype(f32)).astype(bf16)
        ret_a[i, :, HALF : HALF + 128] = jnp.where(
            lane == 0, high.astype(f32), low.astype(f32)).astype(bf16)

    def row_grads(c, dst):
        @pl.loop(0, 4)
        def _(j):
            wrows = pl.ds(pl.multiple_of((j % 2) * 256, 256), 256)
            cols = pl.ds(pl.multiple_of(j * 256, 256), 256)
            out = lax.dot_general(
                d_pre[...], w_full[2 * c + j // 2, wrows, 0 : 2 * HID],
                (((1,), (1,)), ((), ())), preferred_element_type=f32)
            dst[:, :, cols] = (out * SCALE_IN).astype(bf16).reshape(GROUP, BLK, 256)

    row_grads(0, ret_a)
    back_xy_a = xy_stage(ret_a, rxy_a, rxs.at[0], rxr.at[0])
    row_grads(1, ret_b)
    back_xy_b = xy_stage(ret_b, rxy_b, rxs.at[1], rxr.at[1])
    rxy_a[p] = ret_a[p]
    rxy_b[p] = ret_b[p]

    def part_grads(b):
        c = b // 2

        @pl.loop(0, 2)
        def _(i):
            cols = pl.ds(pl.multiple_of((b % 2) * OWN + i * 256, 256), 256)
            rows = pl.ds(pl.multiple_of(i * 256, 256), 256)
            xb = xy_recv[c, :, :, cols].reshape(ROWS, 256)
            db = xy_recv[c + 2, :, :, cols].reshape(ROWS, 256)
            dims = (((0,), (0,)), ((), ()))
            for h in range(2):
                out = lax.dot_general(
                    xb, d_pre[:, h * HID : (h + 1) * HID], dims, preferred_element_type=f32)
                g_part[b, rows, h * HID : (h + 1) * HID] = (out * SCALE_IN).astype(bf16)
            out = lax.dot_general(db, active[...], dims, preferred_element_type=f32)
            g_part[b, rows, 2 * HID : 3 * HID] = (out * SCALE_OUT).astype(bf16)

    part_grads(diag_mate)
    g_c1 = start(remote(g_part.at[diag_mate], c_recv.at[1], gs.at[0], gr.at[0], (e, core_mate)))
    part_grads(core_mate)
    g_c0 = start(remote(g_part.at[core_mate], c_recv.at[0], gs.at[1], gr.at[1], (e, core_mate)))
    part_grads(y_mate)

    def pass_back(xy, src, dst, out, width, i):
        for cp in xy:
            cp.wait_recv()
        permute(src, dst, width, False)
        cps = z_stage(dst, out, rzs.at[i], rzr.at[i])
        out[z] = dst[z]
        return cps

    back_z_a = pass_back(back_xy_a, rxy_a, rz_a, back_a, HALF + 128, 0)

    g_c1.wait_recv()

    @pl.loop(0, OWN // 32)
    def _(i):
        rows = pl.ds(pl.multiple_of(i * 32, 32), 32)
        g_send[rows, :] = (
            g_part[y_mate, rows, :].astype(f32) + c_recv[1, rows, :].astype(f32)).astype(bf16)

    g_y = start(remote(g_send, g_recv, gs.at[2], gr.at[2], (e, y_mate)))

    back_z_b = pass_back(back_xy_b, rxy_b, rz_b, back_b, HALF, 1)
    v_x = send_moment(1, v_in, v_bf, v_recv)

    part_grads(dp)
    g_c0.wait_recv()

    @pl.loop(0, OWN // 32)
    def _(i):
        rows = pl.ds(pl.multiple_of(i * 32, 32), 32)
        g_sum[rows, :] = g_part[dp, rows, :].astype(f32) + c_recv[0, rows, :].astype(f32)

    def collect(cps, src, base):
        for cp in cps:
            cp.wait_recv()

        @pl.loop(0, HALF // 256)
        def _(i):
            cols = pl.ds(pl.multiple_of(i * 256, 256), 256)
            ocols = pl.ds(pl.multiple_of(base + i * 256, 256), 256)
            out = lax.dot_general(
                pick[...], src[:, :, cols].reshape(ROWS, 256),
                (((0,), (0,)), ((), ())), preferred_element_type=f32)
            tg[:, ocols] = out.astype(bf16)

    collect(back_z_a, back_a, 0)
    score_out[...] = back_a[:, :, HALF : HALF + 128].reshape(ROWS, 128)
    collect(back_z_b, back_b, HALF)
    m_x.wait_recv()
    g_y.wait_recv()
    v_x.wait_recv()
    for cp in copies:
        cp.wait_send()


def run_step(*args):
    vm = pl.BlockSpec(memory_space=pltpu.VMEM)
    hbm = pl.BlockSpec(memory_space=pl.ANY)
    own = (OWN, 3 * HID)
    dma = pltpu.SemaphoreType.DMA
    return pl.pallas_call(
        step_kernel,
        name="expert_step",
        out_shape=(
            jax.ShapeDtypeStruct((TOK, D), bf16),
            jax.ShapeDtypeStruct((ROWS, 128), bf16),
            jax.ShapeDtypeStruct(own, f32),
            jax.ShapeDtypeStruct(own, bf16),
            jax.ShapeDtypeStruct(own, bf16),
            jax.ShapeDtypeStruct(own, bf16),
            jax.ShapeDtypeStruct(own, bf16),
        ),
        in_specs=[vm] * 8 + [hbm] * 2,
        out_specs=(vm, vm, vm, vm, vm, hbm, hbm),
        scratch_shapes=[
            pltpu.VMEM((4, GROUP, BLK, HALF), bf16),
            pltpu.VMEM((4, GROUP, BLK, HALF), bf16),
            pltpu.VMEM((4, GROUP, BLK, HALF), bf16),
            pltpu.VMEM((4, GROUP, BLK, HALF), bf16),
            pltpu.VMEM((4,) + own, bf16),
            pltpu.VMEM((GROUP, 8, ROWS), f32),
            pltpu.VMEM((ROWS, ROWS), bf16),
            pltpu.VMEM((ROWS, 2 * HID), bf16),
            pltpu.VMEM((ROWS, HID), f32),
            pltpu.VMEM((ROWS, HID), bf16),
            pltpu.VMEM((ROWS, 2 * HID), bf16),
        ]
        + [pltpu.VMEM((GROUP, BLK, n), bf16) for n in (HALF + 128, HALF) * 4]
        + [
            pltpu.VMEM((4,) + own, bf16),
            pltpu.VMEM((2,) + own, bf16),
            pltpu.VMEM(own, bf16),
            pltpu.VMEM((2,) + own, f32),
            pltpu.VMEM(own, bf16),
            pltpu.VMEM(own, bf16),
            dma((4, 7)), dma((4, 7)), dma((4, 7)), dma((4, 7)),
            dma((7,)), dma((7,)),
            dma((2, 7)), dma((2, 7)), dma((2, 7)), dma((2, 7)),
            dma((4,)), dma((4,)), dma((2,)), dma((2,)), dma((3,)), dma((3,)), dma((2,)),
        ],
        compiler_params=pltpu.CompilerParams(
            collective_id=0, has_side_effects=True, vmem_limit_bytes=62 << 20),
    )(*args)


def per_device(
    tokens, cotangent, expert_ids, gate_probs, weights, first_moment, second_moment, swap_flags
):
    traded = swap_flags[0] != 0
    ids = expert_ids.T
    flat = ids.reshape(-1)
    n = flat.shape[0]
    order = jnp.arange(n, dtype=jnp.int32)
    same = (flat[:, None] == flat[None, :]) & (order[:, None] < order[None, :])
    slot = jnp.sum(same.astype(jnp.int32), axis=0).reshape(ids.shape)
    ex, ez, ey = ids // (NZ * NY), (ids // NY) % NZ, ids % NY
    place = (ez * GROUP + ex * NY + ey) * CAP + slot
    row = jnp.arange(ROWS, dtype=jnp.int32)[:, None]
    hit0 = row == place[0][None, :]
    hit1 = row == place[1][None, :]
    probs = gate_probs.T.astype(f32)
    pick = (hit0 | hit1).astype(bf16)
    pick_prob = (
        jnp.where(hit0, probs[0][None, :], 0.0) + jnp.where(hit1, probs[1][None, :], 0.0)
    ).astype(bf16)

    out_i = jnp.arange(ROWS, dtype=jnp.int32)[:, None]
    in_j = jnp.arange(ROWS, dtype=jnp.int32)[None, :]
    pos, src, s = out_i // BLK, (out_i % BLK) // CAP, out_i % CAP
    plain = (in_j == src * BLK + pos * CAP + s).astype(bf16)
    swapped = (pos + GROUP // 2) % GROUP
    trade = (in_j == src * BLK + swapped * CAP + s).astype(bf16)
    flag = jnp.broadcast_to(traded.astype(f32), (8, 3 * HID))

    token_grads, scores, g_sum, g_recv, w_recv, m_recv, v_recv = run_step(
        pick, pick_prob, tokens, cotangent, weights[0], flag, plain, trade,
        first_moment[0], second_moment[0])

    score = scores[:, 0].astype(f32) + scores[:, 1].astype(f32)
    picked = jnp.sum(
        jnp.where(place[:, :, None] == jnp.arange(ROWS)[None, None, :], score[None, None, :], 0.0),
        axis=2)
    gate_grads = (picked / probs).T.astype(bf16)

    grads = g_sum + g_recv.astype(f32)
    old = jnp.where(traded, w_recv, weights[0]).astype(f32)
    first = jnp.where(traded, m_recv.astype(f32), first_moment[0])
    second = jnp.where(traded, v_recv.astype(f32), second_moment[0])
    moment = 0.9 * first + 0.1 * grads
    square = 0.95 * second + 0.05 * grads * grads
    update = moment / bias_first / (jnp.sqrt(square / bias_second) + 1e-08)
    fresh = (old - 0.02 * (update + 0.1 * old)).astype(bf16)
    return (token_grads, gate_grads, fresh[None], moment[None], square[None])


def solution(mesh):
    tok_spec = P(("expert", "dp"), None)
    row_spec = P("expert", "dp", None)
    return jax.shard_map(
        per_device,
        mesh=mesh,
        in_specs=(tok_spec,) * 4 + (row_spec,) * 3 + (P("expert"),),
        out_specs=(tok_spec,) * 2 + (row_spec,) * 3,
        check_vma=False,
    )
```

```python
import math

import jax
import jax.numpy as jnp
from jax import lax
from jax.experimental import pallas as pl
from jax.experimental.pallas import tpu as pltpu
from jax.sharding import PartitionSpec as P

bias_first = 1.0 - 0.9**20
bias_second = 1.0 - 0.95**20
MESH = pl.DeviceIdType.MESH
f32 = jnp.float32
bf16 = jnp.bfloat16

NX, NZ, NY = 4, 8, 2
CAP = 6
GROUP = 8
SLOTS = (4, 2)
BLKS = tuple(GROUP * n for n in SLOTS)
PROWS = tuple(GROUP * n for n in BLKS)
BASE = (0, PROWS[0])
ROWS = sum(PROWS)
D = 2048
HID = 384
TOK = 128
HALF = 1024
OWN = 512
SCALE_IN = 1.0 / math.sqrt(D)
SCALE_OUT = 1.0 / math.sqrt(HID)
Z_ORDER = (4, 3, 5, 2, 6, 1, 7)
XY_ORDER = ((2, 1), (2, 0), (1, 1), (3, 1), (1, 0), (3, 0), (0, 1))


def step_kernel(
    pick, pick_prob, tok, cot, w_own, flag, plain0, trade0, plain1, trade1, m_hbm, v_hbm,
    tg, score_out, g_sum, g_recv, w_recv, m_recv, v_recv,
    z_send0, z_recv0, xy_send0, xy_recv0, z_send1, z_recv1, xy_send1, xy_recv1,
    w_full, flags, perm0, perm1,
    pre, d_act, active, d_pre,
    ret_a, ret_b, ret_c, rxy_a, rxy_b, rxy_c, rz_a, rz_b, rz_c, back_a, back_b, back_c,
    g_part, c_recv, g_send, stage, m_bf, v_bf,
    zs, zr, xs, xr, fs, fr, rxs, rxr, rzs, rzr, ws, wr, ms, mr, gs, gr, ls,
):
    e = lax.axis_index("expert")
    dp = lax.axis_index("dp")
    x = e // (NZ * NY)
    z = (e // NY) % NZ
    y = e % NY
    p = x * NY + y
    core_mate = dp + 1 - 2 * (dp % 2)
    y_mate = (dp + 2) % 4
    diag_mate = (core_mate + 2) % 4

    def at(nx, nz, ny, nd):
        return (nx * (NZ * NY) + nz * NY + ny, nd)

    def z_dev(k):
        return at(x, (z + k) % NZ, y, dp)

    def xy_pos(k, ky):
        return (x + k) % NX, (y + ky) % NY

    def xy_dev(k, ky):
        nx, ny = xy_pos(k, ky)
        return at(nx, z, ny, dp)

    partner = at((x + 2) % NX, z, y, dp)
    z_send, z_recv = (z_send0, z_send1), (z_recv0, z_recv1)
    xy_send, xy_recv = (xy_send0, xy_send1), (xy_recv0, xy_recv1)
    plain, trade, perm = (plain0, plain1), (trade0, trade1), (perm0, perm1)

    def remote(src, dst, ssem, rsem, device):
        return pltpu.make_async_remote_copy(
            src_ref=src, dst_ref=dst, send_sem=ssem, recv_sem=rsem,
            device_id=device, device_id_type=MESH,
        )

    m_in = pltpu.make_async_copy(m_hbm, stage.at[0], ls.at[0])
    v_in = pltpu.make_async_copy(v_hbm, stage.at[1], ls.at[1])
    m_in.start()
    v_in.start()

    barrier = pltpu.get_barrier_semaphore()
    targets = [z_dev(k) for k in Z_ORDER]
    targets += [xy_dev(*k) for k in XY_ORDER]
    targets += [(e, core_mate), (e, y_mate)]
    for device in targets:
        pl.semaphore_signal(barrier, inc=1, device_id=device, device_id_type=MESH)

    def fill(g, c):
        sel = pick if c == 0 else pick_prob
        src = tok if c == 0 else cot

        @pl.loop(0, D // 256)
        def _(i):
            cols = pl.ds(pl.multiple_of(i * 256, 256), 256)
            out = jnp.dot(
                sel[pl.ds(BASE[g], PROWS[g]), :], src[:, cols], preferred_element_type=f32)
            z_send[g][c, :, :, cols] = out.astype(bf16).reshape(GROUP, BLKS[g], 256)

    fill(0, 0)
    pl.semaphore_wait(barrier, len(targets))

    copies = []

    def start(c):
        c.start()
        copies.append(c)
        return c

    def z_stage(src, dst, ssem, rsem):
        out = []
        for i, k in enumerate(Z_ORDER):
            out.append(start(remote(
                src.at[(z + k) % NZ], dst.at[z], ssem.at[i], rsem.at[i], z_dev(k))))
        return out

    def xy_stage(src, dst, ssem, rsem):
        out = []
        for i, k in enumerate(XY_ORDER):
            nx, ny = xy_pos(*k)
            out.append(start(remote(
                src.at[nx * NY + ny], dst.at[p], ssem.at[i], rsem.at[i], xy_dev(*k))))
        return out

    z_copies = {}

    def send(g, c):
        z_copies[g, c] = z_stage(
            z_send[g].at[c], z_recv[g].at[c], zs.at[2 * g + c], zr.at[2 * g + c])

    send(0, 0)
    w_x = start(remote(w_own, w_recv, ws.at[0], wr.at[0], partner))
    flag_copies = []
    for i, k in enumerate(XY_ORDER):
        flag_copies.append(start(remote(
            flag.at[:, pl.ds(0, PROWS[0])], flags.at[p], fs.at[i], fr.at[i], xy_dev(*k))))
    for g, c in ((0, 1), (1, 0), (1, 1)):
        fill(g, c)
        send(g, c)

    flags[p] = flag[:, pl.ds(0, PROWS[0])]
    for g in range(2):
        for c in range(2):
            z_recv[g][c, z] = z_send[g][c, z]
    for c in flag_copies:
        c.wait_recv()
    for g in range(2):
        for q in range(GROUP):
            rows = pl.ds(q * BLKS[g], BLKS[g])
            f = flags[q, 0:1, 0 : PROWS[g]]
            a = plain[g][rows, :].astype(f32)
            b = trade[g][rows, :].astype(f32)
            perm[g][rows, :] = (a + (b - a) * f).astype(bf16)

    def permute(g, src, dst, width, forward):
        dims = ((1,), (0,)) if forward else ((0,), (0,))

        def tile(start_col, n):
            cols = pl.ds(start_col, n)
            block = src[:, :, cols].reshape(PROWS[g], n)
            out = lax.dot_general(
                perm[g][...], block, (dims, ((), ())), preferred_element_type=f32)
            dst[:, :, cols] = out.astype(bf16).reshape(GROUP, BLKS[g], n)

        @pl.loop(0, width // 256)
        def _(i):
            tile(pl.multiple_of(i * 256, 256), 256)

        if width % 256:
            tile(width - width % 256, width % 256)

    xy_copies = {}

    def dispatch(g, c):
        for cp in z_copies[g, c]:
            cp.wait_recv()
        permute(g, z_recv[g].at[c], xy_send[g].at[c], D, True)
        xy_copies[g, c] = xy_stage(
            xy_send[g].at[c], xy_recv[g].at[c], xs.at[2 * g + c], xr.at[2 * g + c])
        xy_recv[g][c, p] = xy_send[g][c, p]

    dispatch(0, 0)

    w_x.wait_recv()

    @pl.loop(0, OWN // 32)
    def _(i):
        rows = pl.ds(pl.multiple_of(i * 32, 32), 32)
        f = flag[0:1, :]
        mine = w_own[rows, :].astype(f32)
        other = w_recv[rows, :].astype(f32)
        w_full[dp, rows, :] = jnp.where(f != 0.0, other, mine).astype(bf16)

    w_y = start(remote(w_full.at[dp], w_full.at[dp], ws.at[1], wr.at[1], (e, y_mate)))
    w_c = start(remote(w_full.at[dp], w_full.at[dp], ws.at[2], wr.at[2], (e, core_mate)))

    def send_moment(slot, base, n, sem, buf, dst):
        @pl.loop(0, n // 32)
        def _(i):
            rows = pl.ds(pl.multiple_of(base + i * 32, 32), 32)
            buf[rows, :] = stage[slot, rows, :].astype(bf16)

        part = pl.ds(base, n)
        return start(remote(buf.at[part], dst.at[part], ms.at[sem], mr.at[sem], partner))

    m_in.wait()
    m_x0 = send_moment(0, 0, OWN // 2, 0, m_bf, m_recv)
    dispatch(0, 1)
    dispatch(1, 0)
    w_y.wait_recv()
    w_f = start(remote(w_full.at[y_mate], w_full.at[y_mate], ws.at[3], wr.at[3], (e, core_mate)))
    w_c.wait_recv()
    w_f.wait_recv()

    def activate(g):
        for cp in xy_copies[g, 0]:
            cp.wait_recv()
        part = pl.ds(BASE[g], PROWS[g])

        @pl.loop(0, 3)
        def _(i):
            cols = pl.ds(pl.multiple_of(i * 256, 256), 256)
            acc = jnp.zeros((PROWS[g], 256), f32)
            for b in range(4):
                block = xy_recv[g][0, :, :, b * OWN : (b + 1) * OWN].reshape(PROWS[g], OWN)
                acc += jnp.dot(block, w_full[b, :, cols], preferred_element_type=f32)
            pre[part, cols] = (acc * SCALE_IN).astype(bf16)

        @pl.loop(0, PROWS[g] // 64)
        def _(i):
            rows = pl.ds(pl.multiple_of(BASE[g] + i * 64, 64), 64)
            gate = pre[rows, 0:HID].astype(f32)
            u = pre[rows, HID : 2 * HID].astype(f32)
            s = 1.0 / (1.0 + jnp.exp(-gate))
            active[rows, :] = (gate * s * u).astype(bf16)

    def backward(g, score_dst):
        for cp in xy_copies[g, 1]:
            cp.wait_recv()
        blk = BLKS[g]
        lane = lax.broadcasted_iota(jnp.int32, (blk, 128), 1)

        @pl.loop(0, PROWS[g] // 128)
        def _(r):
            acc = jnp.zeros((128, HID), f32)
            n = 128 // blk
            for b in range(4):
                block = xy_recv[g][1, pl.ds(r * n, n), :, b * OWN : (b + 1) * OWN]
                acc += jnp.dot(
                    block.reshape(128, OWN), w_full[b, :, 2 * HID : 3 * HID],
                    preferred_element_type=f32)
            d_act[pl.ds(pl.multiple_of(BASE[g] + r * 128, 128), 128), :] = acc

        @pl.loop(0, GROUP)
        def _(i):
            rows = pl.ds(pl.multiple_of(BASE[g] + i * blk, blk), blk)
            gate = pre[rows, 0:HID].astype(f32)
            u = pre[rows, HID : 2 * HID].astype(f32)
            s = 1.0 / (1.0 + jnp.exp(-gate))
            da = d_act[rows, :] * SCALE_OUT
            sc = jnp.sum(active[rows, :].astype(f32) * da, axis=1, keepdims=True)
            d_pre[rows, 0:HID] = (da * u * s * (1.0 + gate * (1.0 - s))).astype(bf16)
            d_pre[rows, HID : 2 * HID] = (da * gate * s).astype(bf16)
            high = jnp.broadcast_to(sc, (blk, 128)).astype(bf16)
            low = (jnp.broadcast_to(sc, (blk, 128)) - high.astype(f32)).astype(bf16)
            score_dst[i, :, score_dst.shape[2] - 128 : score_dst.shape[2]] = jnp.where(
                lane == 0, high.astype(f32), low.astype(f32)).astype(bf16)

    def row_grads(g, first, n, dst):
        @pl.loop(0, n)
        def _(j):
            k = first + j
            wrows = pl.ds(pl.multiple_of((k % 2) * 256, 256), 256)
            cols = pl.ds(pl.multiple_of(j * 256, 256), 256)
            out = lax.dot_general(
                d_pre[pl.ds(BASE[g], PROWS[g]), :], w_full[k // 2, wrows, 0 : 2 * HID],
                (((1,), (1,)), ((), ())), preferred_element_type=f32)
            dst[:, :, cols] = (out * SCALE_IN).astype(bf16).reshape(GROUP, BLKS[g], 256)

    def back_xy(src, dst, i):
        cps = xy_stage(src, dst, rxs.at[i], rxr.at[i])
        dst[p] = src[p]
        return cps

    activate(0)
    dispatch(1, 1)
    backward(0, ret_a)
    row_grads(0, 0, 4, ret_a)
    back_xy_a = back_xy(ret_a, rxy_a, 0)
    row_grads(0, 4, 4, ret_b)
    back_xy_b = back_xy(ret_b, rxy_b, 1)
    activate(1)
    backward(1, ret_c)
    row_grads(1, 0, 8, ret_c)
    back_xy_c = back_xy(ret_c, rxy_c, 2)
    m_x1 = send_moment(0, OWN // 2, OWN // 2, 1, m_bf, m_recv)
    v_in.wait()
    v_x = send_moment(1, 0, OWN, 2, v_bf, v_recv)

    def part_grads(b):
        dims = (((0,), (0,)), ((), ()))

        def both(c, cols, rhs, rcols):
            out = None
            for g in range(2):
                lhs = xy_recv[g][c, :, :, cols].reshape(PROWS[g], 256)
                dot = lax.dot_general(
                    lhs, rhs[BASE[g] : BASE[g] + PROWS[g], rcols], dims,
                    preferred_element_type=f32)
                out = dot if out is None else out + dot
            return out

        @pl.loop(0, 2)
        def _(i):
            cols = pl.ds(pl.multiple_of(b * OWN + i * 256, 256), 256)
            rows = pl.ds(pl.multiple_of(i * 256, 256), 256)
            for h in range(2):
                hcols = slice(h * HID, (h + 1) * HID)
                g_part[b, rows, hcols] = (both(0, cols, d_pre, hcols) * SCALE_IN).astype(bf16)
            out = both(1, cols, active, slice(0, HID))
            g_part[b, rows, 2 * HID : 3 * HID] = (out * SCALE_OUT).astype(bf16)

    def pass_back(g, xy, src, dst, out, width, i):
        for cp in xy:
            cp.wait_recv()
        permute(g, src, dst, width, False)
        cps = z_stage(dst, out, rzs.at[i], rzr.at[i])
        out[z] = dst[z]
        return cps

    part_grads(diag_mate)
    g_c1 = start(remote(g_part.at[diag_mate], c_recv.at[1], gs.at[0], gr.at[0], (e, core_mate)))
    back_z_a = pass_back(0, back_xy_a, rxy_a, rz_a, back_a, HALF + 128, 0)
    part_grads(y_mate)
    g_c1.wait_recv()

    @pl.loop(0, OWN // 32)
    def _(i):
        rows = pl.ds(pl.multiple_of(i * 32, 32), 32)
        g_send[rows, :] = (
            g_part[y_mate, rows, :].astype(f32) + c_recv[1, rows, :].astype(f32)).astype(bf16)

    g_y = start(remote(g_send, g_recv, gs.at[2], gr.at[2], (e, y_mate)))
    back_z_b = pass_back(0, back_xy_b, rxy_b, rz_b, back_b, HALF, 1)
    back_z_c = pass_back(1, back_xy_c, rxy_c, rz_c, back_c, D + 128, 2)
    part_grads(core_mate)
    g_c0 = start(remote(g_part.at[core_mate], c_recv.at[0], gs.at[1], gr.at[1], (e, core_mate)))
    part_grads(dp)
    g_c0.wait_recv()

    @pl.loop(0, OWN // 32)
    def _(i):
        rows = pl.ds(pl.multiple_of(i * 32, 32), 32)
        g_sum[rows, :] = g_part[dp, rows, :].astype(f32) + c_recv[0, rows, :].astype(f32)

    for cps in (back_z_a, back_z_b, back_z_c):
        for cp in cps:
            cp.wait_recv()

    def collect(src, base):
        @pl.loop(0, HALF // 256)
        def _(i):
            cols = pl.ds(pl.multiple_of(i * 256, 256), 256)
            ocols = pl.ds(pl.multiple_of(base + i * 256, 256), 256)
            dims = (((0,), (0,)), ((), ()))
            out = lax.dot_general(
                pick[0 : PROWS[0], :], src[:, :, cols].reshape(PROWS[0], 256), dims,
                preferred_element_type=f32)
            out += lax.dot_general(
                pick[PROWS[0] : ROWS, :], back_c[:, :, ocols].reshape(PROWS[1], 256), dims,
                preferred_element_type=f32)
            tg[:, ocols] = out.astype(bf16)

    collect(back_a, 0)
    collect(back_b, HALF)
    score_out[0 : PROWS[0], :] = back_a[:, :, HALF : HALF + 128].reshape(PROWS[0], 128)
    score_out[PROWS[0] : ROWS, :] = back_c[:, :, D : D + 128].reshape(PROWS[1], 128)
    m_x0.wait_recv()
    m_x1.wait_recv()
    g_y.wait_recv()
    v_x.wait_recv()
    for cp in copies:
        cp.wait_send()


def run_step(*args):
    vm = pl.BlockSpec(memory_space=pltpu.VMEM)
    hbm = pl.BlockSpec(memory_space=pl.ANY)
    own = (OWN, 3 * HID)
    dma = pltpu.SemaphoreType.DMA
    return pl.pallas_call(
        step_kernel,
        name="expert_step",
        out_shape=(
            jax.ShapeDtypeStruct((TOK, D), bf16),
            jax.ShapeDtypeStruct((ROWS, 128), bf16),
            jax.ShapeDtypeStruct(own, f32),
            jax.ShapeDtypeStruct(own, bf16),
            jax.ShapeDtypeStruct(own, bf16),
            jax.ShapeDtypeStruct(own, bf16),
            jax.ShapeDtypeStruct(own, bf16),
        ),
        in_specs=[vm] * 10 + [hbm] * 2,
        out_specs=(vm, vm, vm, vm, vm, hbm, hbm),
        scratch_shapes=[
            pltpu.VMEM((2, GROUP, blk, D), bf16) for blk in BLKS for _ in range(4)
        ]
        + [
            pltpu.VMEM((4,) + own, bf16),
            pltpu.VMEM((GROUP, 8, PROWS[0]), f32),
            pltpu.VMEM((PROWS[0], PROWS[0]), bf16),
            pltpu.VMEM((PROWS[1], PROWS[1]), bf16),
            pltpu.VMEM((ROWS, 2 * HID), bf16),
            pltpu.VMEM((ROWS, HID), f32),
            pltpu.VMEM((ROWS, HID), bf16),
            pltpu.VMEM((ROWS, 2 * HID), bf16),
        ]
        + [
            pltpu.VMEM((GROUP,) + shape, bf16)
            for shape in ((BLKS[0], HALF + 128), (BLKS[0], HALF), (BLKS[1], D + 128)) * 4
        ]
        + [
            pltpu.VMEM((4,) + own, bf16),
            pltpu.VMEM((2,) + own, bf16),
            pltpu.VMEM(own, bf16),
            pltpu.VMEM((2,) + own, f32),
            pltpu.VMEM(own, bf16),
            pltpu.VMEM(own, bf16),
            dma((4, 7)), dma((4, 7)), dma((4, 7)), dma((4, 7)),
            dma((7,)), dma((7,)),
            dma((3, 7)), dma((3, 7)), dma((3, 7)), dma((3, 7)),
            dma((4,)), dma((4,)), dma((3,)), dma((3,)), dma((3,)), dma((3,)), dma((2,)),
        ],
        compiler_params=pltpu.CompilerParams(
            collective_id=0, has_side_effects=True, vmem_limit_bytes=62 << 20),
    )(*args)


def per_device(
    tokens, cotangent, expert_ids, gate_probs, weights, first_moment, second_moment, swap_flags
):
    traded = swap_flags[0] != 0
    ids = expert_ids.T
    flat = ids.reshape(-1)
    n = flat.shape[0]
    order = jnp.arange(n, dtype=jnp.int32)
    same = (flat[:, None] == flat[None, :]) & (order[:, None] < order[None, :])
    slot = jnp.sum(same.astype(jnp.int32), axis=0).reshape(ids.shape)
    ex, ez, ey = ids // (NZ * NY), (ids // NY) % NZ, ids % NY
    spot = ez * GROUP + ex * NY + ey
    place = jnp.where(
        slot < SLOTS[0], spot * SLOTS[0] + slot, BASE[1] + spot * SLOTS[1] + slot - SLOTS[0])
    row = jnp.arange(ROWS, dtype=jnp.int32)[:, None]
    hit0 = row == place[0][None, :]
    hit1 = row == place[1][None, :]
    probs = gate_probs.T.astype(f32)
    pick = (hit0 | hit1).astype(bf16)
    pick_prob = (
        jnp.where(hit0, probs[0][None, :], 0.0) + jnp.where(hit1, probs[1][None, :], 0.0)
    ).astype(bf16)

    moves = []
    for n, blk, rows in zip(SLOTS, BLKS, PROWS):
        out_i = jnp.arange(rows, dtype=jnp.int32)[:, None]
        in_j = jnp.arange(rows, dtype=jnp.int32)[None, :]
        pos, src, s = out_i // blk, (out_i % blk) // n, out_i % n
        moves.append((in_j == src * blk + pos * n + s).astype(bf16))
        swapped = (pos + GROUP // 2) % GROUP
        moves.append((in_j == src * blk + swapped * n + s).astype(bf16))
    flag = jnp.broadcast_to(traded.astype(f32), (8, 3 * HID))

    token_grads, scores, g_sum, g_recv, w_recv, m_recv, v_recv = run_step(
        pick, pick_prob, tokens, cotangent, weights[0], flag, *moves,
        first_moment[0], second_moment[0])

    score = scores[:, 0].astype(f32) + scores[:, 1].astype(f32)
    picked = jnp.sum(
        jnp.where(place[:, :, None] == jnp.arange(ROWS)[None, None, :], score[None, None, :], 0.0),
        axis=2)
    gate_grads = (picked / probs).T.astype(bf16)

    grads = g_sum + g_recv.astype(f32)
    old = jnp.where(traded, w_recv, weights[0]).astype(f32)
    first = jnp.where(traded, m_recv.astype(f32), first_moment[0])
    second = jnp.where(traded, v_recv.astype(f32), second_moment[0])
    moment = 0.9 * first + 0.1 * grads
    square = 0.95 * second + 0.05 * grads * grads
    update = moment / bias_first / (jnp.sqrt(square / bias_second) + 1e-08)
    fresh = (old - 0.02 * (update + 0.1 * old)).astype(bf16)
    return (token_grads, gate_grads, fresh[None], moment[None], square[None])


def solution(mesh):
    tok_spec = P(("expert", "dp"), None)
    row_spec = P("expert", "dp", None)
    return jax.shard_map(
        per_device,
        mesh=mesh,
        in_specs=(tok_spec,) * 4 + (row_spec,) * 3 + (P("expert"),),
        out_specs=(tok_spec,) * 2 + (row_spec,) * 3,
        check_vma=False,
    )
```

```python
import math

import jax
import jax.numpy as jnp
from jax import lax
from jax.experimental import pallas as pl
from jax.experimental.pallas import tpu as pltpu
from jax.sharding import PartitionSpec as P

bias_first = 1.0 - 0.9**20
bias_second = 1.0 - 0.95**20
MESH = pl.DeviceIdType.MESH
f32 = jnp.float32
bf16 = jnp.bfloat16

NX, NZ, NY = 4, 8, 2
CAP = 6
GROUP = 8
BLK = GROUP * CAP
ROWS = GROUP * BLK
D = 2048
HID = 384
TOK = 128
HALF = 1024
OWN = 512
SCALE_IN = 1.0 / math.sqrt(D)
SCALE_OUT = 1.0 / math.sqrt(HID)
Z_ORDER = (4, 3, 5, 2, 6, 1, 7)
XY_ORDER = ((2, 1), (2, 0), (1, 1), (3, 1), (1, 0), (3, 0), (0, 1))


def step_kernel(
    pick, pick_prob, tok, cot, w_own, flag, plain, trade, m_hbm, v_hbm,
    tg, score_out, g_sum, g_recv, w_recv, m_recv, v_recv,
    z_send, z_recv, xy_send, xy_recv, w_full, flags, perm,
    pre, d_act, active, d_pre,
    ret_a, ret_b, rxy_a, rxy_b, rz_a, rz_b, back_a, back_b,
    g_part, c_recv, g_send, stage, m_bf, v_bf,
    zs, zr, xs, xr, fs, fr, rxs, rxr, rzs, rzr, ws, wr, ms, mr, gs, gr, ls,
):
    e = lax.axis_index("expert")
    dp = lax.axis_index("dp")
    x = e // (NZ * NY)
    z = (e // NY) % NZ
    y = e % NY
    p = x * NY + y
    core_mate = dp + 1 - 2 * (dp % 2)
    y_mate = (dp + 2) % 4
    diag_mate = (core_mate + 2) % 4

    def at(nx, nz, ny, nd):
        return (nx * (NZ * NY) + nz * NY + ny, nd)

    def z_dev(k):
        return at(x, (z + k) % NZ, y, dp)

    def xy_pos(k, ky):
        return (x + k) % NX, (y + ky) % NY

    def xy_dev(k, ky):
        nx, ny = xy_pos(k, ky)
        return at(nx, z, ny, dp)

    partner = at((x + 2) % NX, z, y, dp)

    def remote(src, dst, ssem, rsem, device):
        return pltpu.make_async_remote_copy(
            src_ref=src, dst_ref=dst, send_sem=ssem, recv_sem=rsem,
            device_id=device, device_id_type=MESH,
        )

    m_in = pltpu.make_async_copy(m_hbm, stage.at[0], ls.at[0])
    v_in = pltpu.make_async_copy(v_hbm, stage.at[1], ls.at[1])
    m_in.start()
    v_in.start()

    barrier = pltpu.get_barrier_semaphore()
    targets = [z_dev(k) for k in Z_ORDER]
    targets += [xy_dev(*k) for k in XY_ORDER]
    targets += [(e, core_mate), (e, y_mate)]
    for device in targets:
        pl.semaphore_signal(barrier, inc=1, device_id=device, device_id_type=MESH)

    def fill(c):
        sel = pick if c < 2 else pick_prob
        src = tok if c < 2 else cot

        @pl.loop(0, HALF // 256)
        def _(i):
            cols = pl.ds(pl.multiple_of(i * 256, 256), 256)
            scols = pl.ds(pl.multiple_of((c % 2) * HALF + i * 256, 256), 256)
            out = jnp.dot(sel[...], src[:, scols], preferred_element_type=f32)
            z_send[c, :, :, cols] = out.astype(bf16).reshape(GROUP, BLK, 256)

    fill(0)
    pl.semaphore_wait(barrier, len(targets))

    copies = []

    def start(c):
        c.start()
        copies.append(c)
        return c

    def z_stage(src, dst, ssem, rsem):
        out = []
        for i, k in enumerate(Z_ORDER):
            out.append(start(remote(
                src.at[(z + k) % NZ], dst.at[z], ssem.at[i], rsem.at[i], z_dev(k))))
        return out

    def xy_stage(src, dst, ssem, rsem):
        out = []
        for i, k in enumerate(XY_ORDER):
            nx, ny = xy_pos(*k)
            out.append(start(remote(
                src.at[nx * NY + ny], dst.at[p], ssem.at[i], rsem.at[i], xy_dev(*k))))
        return out

    z_copies = [z_stage(z_send.at[0], z_recv.at[0], zs.at[0], zr.at[0])]
    flag_copies = []
    for i, k in enumerate(XY_ORDER):
        flag_copies.append(start(remote(
            flag.at[:, pl.ds(0, ROWS)], flags.at[p], fs.at[i], fr.at[i], xy_dev(*k))))
    w_x = start(remote(w_own, w_recv, ws.at[0], wr.at[0], partner))
    for c in range(1, 4):
        fill(c)
        z_copies.append(z_stage(z_send.at[c], z_recv.at[c], zs.at[c], zr.at[c]))

    flags[p] = flag[:, pl.ds(0, ROWS)]
    for c in range(4):
        z_recv[c, z] = z_send[c, z]
    for c in flag_copies:
        c.wait_recv()
    for q in range(GROUP):
        rows = pl.ds(q * BLK, BLK)
        f = flags[q, 0:1, :]
        a = plain[rows, :].astype(f32)
        b = trade[rows, :].astype(f32)
        perm[rows, :] = (a + (b - a) * f).astype(bf16)

    def permute(src, dst, width, forward):
        dims = ((1,), (0,)) if forward else ((0,), (0,))

        def tile(start_col, n):
            cols = pl.ds(start_col, n)
            block = src[:, :, cols].reshape(ROWS, n)
            out = lax.dot_general(perm[...], block, (dims, ((), ())), preferred_element_type=f32)
            dst[:, :, cols] = out.astype(bf16).reshape(GROUP, BLK, n)

        @pl.loop(0, width // 256)
        def _(i):
            tile(pl.multiple_of(i * 256, 256), 256)

        if width % 256:
            tile(width - width % 256, width % 256)

    xy_copies = [None] * 4

    def dispatch(c):
        for cp in z_copies[c]:
            cp.wait_recv()
        permute(z_recv.at[c], xy_send.at[c], HALF, True)
        xy_copies[c] = xy_stage(xy_send.at[c], xy_recv.at[c], xs.at[c], xr.at[c])
        xy_recv[c, p] = xy_send[c, p]

    dispatch(0)

    w_x.wait_recv()

    @pl.loop(0, OWN // 32)
    def _(i):
        rows = pl.ds(pl.multiple_of(i * 32, 32), 32)
        f = flag[0:1, :]
        mine = w_own[rows, :].astype(f32)
        other = w_recv[rows, :].astype(f32)
        w_full[dp, rows, :] = jnp.where(f != 0.0, other, mine).astype(bf16)

    w_y = start(remote(w_full.at[dp], w_full.at[dp], ws.at[1], wr.at[1], (e, y_mate)))
    w_c = start(remote(w_full.at[dp], w_full.at[dp], ws.at[2], wr.at[2], (e, core_mate)))

    def send_moment(slot, local, buf, dst):
        local.wait()

        @pl.loop(0, OWN // 32)
        def _(i):
            rows = pl.ds(pl.multiple_of(i * 32, 32), 32)
            buf[rows, :] = stage[slot, rows, :].astype(bf16)

        return start(remote(buf, dst, ms.at[slot], mr.at[slot], partner))

    dispatch(1)
    m_x = send_moment(0, m_in, m_bf, m_recv)
    dispatch(2)
    w_y.wait_recv()
    w_f = start(remote(w_full.at[y_mate], w_full.at[y_mate], ws.at[3], wr.at[3], (e, core_mate)))
    w_c.wait_recv()
    w_f.wait_recv()
    for c in (0, 1):
        for cp in xy_copies[c]:
            cp.wait_recv()

    def x_block(c, cols):
        return xy_recv[c, :, :, cols].reshape(ROWS, cols.size)

    @pl.loop(0, 3)
    def _(i):
        cols = pl.ds(pl.multiple_of(i * 256, 256), 256)
        acc = jnp.zeros((ROWS, 256), f32)
        for b in range(4):
            acc += jnp.dot(
                x_block(b // 2, pl.ds((b % 2) * OWN, OWN)), w_full[b, :, cols],
                preferred_element_type=f32)
        pre[:, cols] = (acc * SCALE_IN).astype(bf16)

    @pl.loop(0, GROUP)
    def _(i):
        rows = pl.ds(pl.multiple_of(i * BLK, BLK), BLK)
        g = pre[rows, 0:HID].astype(f32)
        u = pre[rows, HID : 2 * HID].astype(f32)
        s = 1.0 / (1.0 + jnp.exp(-g))
        active[rows, :] = (g * s * u).astype(bf16)

    dispatch(3)

    def act_part(c):
        for cp in xy_copies[c]:
            cp.wait_recv()

        @pl.loop(0, 2)
        def _(r):
            rows = pl.ds(pl.multiple_of(r * (ROWS // 2), ROWS // 2), ROWS // 2)
            acc = jnp.zeros((ROWS // 2, HID), f32)
            for b in (2 * (c % 2), 2 * (c % 2) + 1):
                block = xy_recv[c, pl.ds(r * 4, 4), :, pl.ds((b % 2) * OWN, OWN)]
                acc += jnp.dot(
                    block.reshape(ROWS // 2, OWN), w_full[b, :, 2 * HID : 3 * HID],
                    preferred_element_type=f32)
            if c == 2:
                d_act[rows, :] = acc
            else:
                d_act[rows, :] += acc

    act_part(2)
    act_part(3)

    lane = lax.broadcasted_iota(jnp.int32, (BLK, 128), 1)

    @pl.loop(0, GROUP)
    def _(i):
        rows = pl.ds(pl.multiple_of(i * BLK, BLK), BLK)
        g = pre[rows, 0:HID].astype(f32)
        u = pre[rows, HID : 2 * HID].astype(f32)
        s = 1.0 / (1.0 + jnp.exp(-g))
        da = d_act[rows, :] * SCALE_OUT
        sc = jnp.sum(active[rows, :].astype(f32) * da, axis=1, keepdims=True)
        d_pre[rows, 0:HID] = (da * u * s * (1.0 + g * (1.0 - s))).astype(bf16)
        d_pre[rows, HID : 2 * HID] = (da * g * s).astype(bf16)
        high = jnp.broadcast_to(sc, (BLK, 128)).astype(bf16)
        low = (jnp.broadcast_to(sc, (BLK, 128)) - high.astype(f32)).astype(bf16)
        ret_a[i, :, HALF : HALF + 128] = jnp.where(
            lane == 0, high.astype(f32), low.astype(f32)).astype(bf16)

    def row_grads(c, dst):
        @pl.loop(0, 4)
        def _(j):
            wrows = pl.ds(pl.multiple_of((j % 2) * 256, 256), 256)
            cols = pl.ds(pl.multiple_of(j * 256, 256), 256)
            out = lax.dot_general(
                d_pre[...], w_full[2 * c + j // 2, wrows, 0 : 2 * HID],
                (((1,), (1,)), ((), ())), preferred_element_type=f32)
            dst[:, :, cols] = (out * SCALE_IN).astype(bf16).reshape(GROUP, BLK, 256)

    row_grads(0, ret_a)
    back_xy_a = xy_stage(ret_a, rxy_a, rxs.at[0], rxr.at[0])
    row_grads(1, ret_b)
    back_xy_b = xy_stage(ret_b, rxy_b, rxs.at[1], rxr.at[1])
    v_x = send_moment(1, v_in, v_bf, v_recv)
    rxy_a[p] = ret_a[p]
    rxy_b[p] = ret_b[p]

    def part_grads(b):
        c = b // 2

        @pl.loop(0, 2)
        def _(i):
            cols = pl.ds(pl.multiple_of((b % 2) * OWN + i * 256, 256), 256)
            rows = pl.ds(pl.multiple_of(i * 256, 256), 256)
            xb = xy_recv[c, :, :, cols].reshape(ROWS, 256)
            db = xy_recv[c + 2, :, :, cols].reshape(ROWS, 256)
            dims = (((0,), (0,)), ((), ()))
            for h in range(2):
                out = lax.dot_general(
                    xb, d_pre[:, h * HID : (h + 1) * HID], dims, preferred_element_type=f32)
                g_part[b, rows, h * HID : (h + 1) * HID] = (out * SCALE_IN).astype(bf16)
            out = lax.dot_general(db, active[...], dims, preferred_element_type=f32)
            g_part[b, rows, 2 * HID : 3 * HID] = (out * SCALE_OUT).astype(bf16)

    part_grads(diag_mate)
    g_c1 = start(remote(g_part.at[diag_mate], c_recv.at[1], gs.at[0], gr.at[0], (e, core_mate)))
    part_grads(core_mate)
    g_c0 = start(remote(g_part.at[core_mate], c_recv.at[0], gs.at[1], gr.at[1], (e, core_mate)))
    part_grads(y_mate)

    def pass_back(xy, src, dst, out, width, i):
        for cp in xy:
            cp.wait_recv()
        permute(src, dst, width, False)
        cps = z_stage(dst, out, rzs.at[i], rzr.at[i])
        out[z] = dst[z]
        return cps

    back_z_a = pass_back(back_xy_a, rxy_a, rz_a, back_a, HALF + 128, 0)

    g_c1.wait_recv()

    @pl.loop(0, OWN // 32)
    def _(i):
        rows = pl.ds(pl.multiple_of(i * 32, 32), 32)
        g_send[rows, :] = (
            g_part[y_mate, rows, :].astype(f32) + c_recv[1, rows, :].astype(f32)).astype(bf16)

    g_y = start(remote(g_send, g_recv, gs.at[2], gr.at[2], (e, y_mate)))

    back_z_b = pass_back(back_xy_b, rxy_b, rz_b, back_b, HALF, 1)

    part_grads(dp)
    g_c0.wait_recv()

    @pl.loop(0, OWN // 32)
    def _(i):
        rows = pl.ds(pl.multiple_of(i * 32, 32), 32)
        g_sum[rows, :] = g_part[dp, rows, :].astype(f32) + c_recv[0, rows, :].astype(f32)

    def collect(cps, src, base):
        for cp in cps:
            cp.wait_recv()

        @pl.loop(0, HALF // 256)
        def _(i):
            cols = pl.ds(pl.multiple_of(i * 256, 256), 256)
            ocols = pl.ds(pl.multiple_of(base + i * 256, 256), 256)
            out = lax.dot_general(
                pick[...], src[:, :, cols].reshape(ROWS, 256),
                (((0,), (0,)), ((), ())), preferred_element_type=f32)
            tg[:, ocols] = out.astype(bf16)

    collect(back_z_a, back_a, 0)
    score_out[...] = back_a[:, :, HALF : HALF + 128].reshape(ROWS, 128)
    collect(back_z_b, back_b, HALF)
    m_x.wait_recv()
    g_y.wait_recv()
    v_x.wait_recv()
    for cp in copies:
        cp.wait_send()


def run_step(*args):
    vm = pl.BlockSpec(memory_space=pltpu.VMEM)
    hbm = pl.BlockSpec(memory_space=pl.ANY)
    own = (OWN, 3 * HID)
    dma = pltpu.SemaphoreType.DMA
    return pl.pallas_call(
        step_kernel,
        name="expert_step",
        out_shape=(
            jax.ShapeDtypeStruct((TOK, D), bf16),
            jax.ShapeDtypeStruct((ROWS, 128), bf16),
            jax.ShapeDtypeStruct(own, f32),
            jax.ShapeDtypeStruct(own, bf16),
            jax.ShapeDtypeStruct(own, bf16),
            jax.ShapeDtypeStruct(own, bf16),
            jax.ShapeDtypeStruct(own, bf16),
        ),
        in_specs=[vm] * 8 + [hbm] * 2,
        out_specs=(vm, vm, vm, vm, vm, hbm, hbm),
        scratch_shapes=[
            pltpu.VMEM((4, GROUP, BLK, HALF), bf16),
            pltpu.VMEM((4, GROUP, BLK, HALF), bf16),
            pltpu.VMEM((4, GROUP, BLK, HALF), bf16),
            pltpu.VMEM((4, GROUP, BLK, HALF), bf16),
            pltpu.VMEM((4,) + own, bf16),
            pltpu.VMEM((GROUP, 8, ROWS), f32),
            pltpu.VMEM((ROWS, ROWS), bf16),
            pltpu.VMEM((ROWS, 2 * HID), bf16),
            pltpu.VMEM((ROWS, HID), f32),
            pltpu.VMEM((ROWS, HID), bf16),
            pltpu.VMEM((ROWS, 2 * HID), bf16),
        ]
        + [pltpu.VMEM((GROUP, BLK, n), bf16) for n in (HALF + 128, HALF) * 4]
        + [
            pltpu.VMEM((4,) + own, bf16),
            pltpu.VMEM((2,) + own, bf16),
            pltpu.VMEM(own, bf16),
            pltpu.VMEM((2,) + own, f32),
            pltpu.VMEM(own, bf16),
            pltpu.VMEM(own, bf16),
            dma((4, 7)), dma((4, 7)), dma((4, 7)), dma((4, 7)),
            dma((7,)), dma((7,)),
            dma((2, 7)), dma((2, 7)), dma((2, 7)), dma((2, 7)),
            dma((4,)), dma((4,)), dma((2,)), dma((2,)), dma((3,)), dma((3,)), dma((2,)),
        ],
        compiler_params=pltpu.CompilerParams(
            collective_id=0, has_side_effects=True, vmem_limit_bytes=62 << 20),
    )(*args)


def per_device(
    tokens, cotangent, expert_ids, gate_probs, weights, first_moment, second_moment, swap_flags
):
    traded = swap_flags[0] != 0
    ids = expert_ids.T
    flat = ids.reshape(-1)
    n = flat.shape[0]
    order = jnp.arange(n, dtype=jnp.int32)
    same = (flat[:, None] == flat[None, :]) & (order[:, None] < order[None, :])
    slot = jnp.sum(same.astype(jnp.int32), axis=0).reshape(ids.shape)
    ex, ez, ey = ids // (NZ * NY), (ids // NY) % NZ, ids % NY
    place = (ez * GROUP + ex * NY + ey) * CAP + slot
    row = jnp.arange(ROWS, dtype=jnp.int32)[:, None]
    hit0 = row == place[0][None, :]
    hit1 = row == place[1][None, :]
    probs = gate_probs.T.astype(f32)
    pick = (hit0 | hit1).astype(bf16)
    pick_prob = (
        jnp.where(hit0, probs[0][None, :], 0.0) + jnp.where(hit1, probs[1][None, :], 0.0)
    ).astype(bf16)

    out_i = jnp.arange(ROWS, dtype=jnp.int32)[:, None]
    in_j = jnp.arange(ROWS, dtype=jnp.int32)[None, :]
    pos, src, s = out_i // BLK, (out_i % BLK) // CAP, out_i % CAP
    plain = (in_j == src * BLK + pos * CAP + s).astype(bf16)
    swapped = (pos + GROUP // 2) % GROUP
    trade = (in_j == src * BLK + swapped * CAP + s).astype(bf16)
    flag = jnp.broadcast_to(traded.astype(f32), (8, 3 * HID))

    token_grads, scores, g_sum, g_recv, w_recv, m_recv, v_recv = run_step(
        pick, pick_prob, tokens, cotangent, weights[0], flag, plain, trade,
        first_moment[0], second_moment[0])

    score = scores[:, 0].astype(f32) + scores[:, 1].astype(f32)
    picked = jnp.sum(
        jnp.where(place[:, :, None] == jnp.arange(ROWS)[None, None, :], score[None, None, :], 0.0),
        axis=2)
    gate_grads = (picked / probs).T.astype(bf16)

    grads = g_sum + g_recv.astype(f32)
    old = jnp.where(traded, w_recv, weights[0]).astype(f32)
    first = jnp.where(traded, m_recv.astype(f32), first_moment[0])
    second = jnp.where(traded, v_recv.astype(f32), second_moment[0])
    moment = 0.9 * first + 0.1 * grads
    square = 0.95 * second + 0.05 * grads * grads
    update = moment / bias_first / (jnp.sqrt(square / bias_second) + 1e-08)
    fresh = (old - 0.02 * (update + 0.1 * old)).astype(bf16)
    return (token_grads, gate_grads, fresh[None], moment[None], square[None])


def solution(mesh):
    tok_spec = P(("expert", "dp"), None)
    row_spec = P("expert", "dp", None)
    return jax.shard_map(
        per_device,
        mesh=mesh,
        in_specs=(tok_spec,) * 4 + (row_spec,) * 3 + (P("expert"),),
        out_specs=(tok_spec,) * 2 + (row_spec,) * 3,
        check_vma=False,
    )
```
